32 devices in a mesh: tm: 8 (over y, x, core), ens: 4 (over z).
Axes of the slice: x: 2, y: 2, z: 4, core: 2. Of those that a mesh axis runs over, the one named last changes fastest.
Arguments:
- dynamics: float32 [32, 256, 256], P('tm'), may hold values from -2 to 2
- precision: float32 [32, 256], P('tm'), may hold values from 0.0005 to 6
- right_side: float32 [32, 32, 256], P('tm', 'ens'), parts along dimension 1, may hold values from -0.1 to 0.1
Outputs:
- solution: float32 [32, 32, 256], P('tm', 'ens'), parts along dimension 1
The draws below stay inside these ranges and needn't reach their ends.
There are 4 independent parts, one for each index of `ens`. The reference program is written for one: setup_inputs(seed, part) draws one part's arguments, and reference() takes and returns one part's arrays. A program takes and returns all parts, laid end to end along the dimension named above; an argument that names none is the same for every part. Nothing has to cross between parts.
All inputs are finite; a program needn't handle non-finite values.
Results may differ from the reference program's by a relative error of at most 0.0003.
Values sent between devices are 32-bit elements; how exact they have to be, the bound alone decides.
No kernel may reach another device: no remote copies, remote signals or barrier semaphores. Data moves between devices by JAX's collectives and lax.ppermute only.
A program may use at most 128 MiB of HBM per device.

```python
import math
import jax
import jax.numpy as jnp
from jax import lax

S = 256
R = 8
TSTEPS = 32


def draw_dynamics(key, part):
    first_key, second_key = jax.random.split(key)
    noise = jnp.clip(jax.random.normal(first_key, (TSTEPS, S, S), jnp.float32), -6.0, 6.0) * (0.2 / math.sqrt(S))
    scales = jax.random.uniform(second_key, (TSTEPS, S), jnp.float32, 0.98, 1.02)
    identity = jnp.eye(S, dtype=jnp.float32)
    return noise + scales[:, :, None] * identity[None]


def draw_precision(key, part):
    first_key, second_key, third_key = jax.random.split(key, 3)
    upper_end = 0.1
    starting_offset = jnp.exp(jax.random.uniform(first_key, (S,), jnp.float32, math.log(0.001), math.log(upper_end)))
    unsmoothed_estimate = jnp.exp(jax.random.uniform(second_key, (TSTEPS, S), jnp.float32, math.log(0.5), math.log(2.0)))
    selected_indices = jax.random.randint(third_key, (TSTEPS,), 0, max(TSTEPS // 4, 2))
    noise_pulses = jnp.where(selected_indices == 0, 30.0, 1.0).astype(jnp.float32)
    return starting_offset[None, :] * unsmoothed_estimate * noise_pulses[:, None]


def draw_right_side(key, part):
    first_key = jax.random.fold_in(key, 0)
    return 0.01 * jnp.clip(jax.random.normal(first_key, (TSTEPS, R, S), jnp.float32), -6.0, 6.0)


def setup_inputs(seed: int = 0, part: int = 0) -> dict:
    keys = jax.random.split(jax.random.key(seed), 4)
    own_keys = jax.random.split(jax.random.fold_in(keys[3], part), 4)
    dynamics = draw_dynamics(jax.random.fold_in(keys[3], 71), part)
    precision = draw_precision(jax.random.fold_in(keys[3], 71), part)
    right_side = draw_right_side(jax.random.fold_in(jax.random.fold_in(keys[3], part), 71), part)
    return dict(dynamics=dynamics, precision=precision, right_side=right_side)


def product(left, right):
    return jnp.dot(left, right, precision=lax.Precision.HIGHEST)

def factor_solve(matrix, columns):
    settled = 0.5 * (matrix + matrix.T)
    factor = jnp.linalg.cholesky(settled)
    return jax.scipy.linalg.cho_solve((factor, True), columns)

def block_thomas(diagonal, below_block, upper_coupling_block, columns):
    state_width = diagonal.shape[1]

    def forward(carried, inputs):
        ratio_before, solved_before = carried
        diag_block, low_block, high_block, column_block = inputs
        schur_block = diag_block - product(low_block, ratio_before)
        combined = factor_solve(schur_block, jnp.concatenate([high_block, column_block - product(low_block, solved_before)], axis=1))
        return ((combined[:, :state_width], combined[:, state_width:]), combined)
    initial = (jnp.zeros_like(diagonal[0]), jnp.zeros_like(columns[0]))
    _, stacked = lax.scan(forward, initial, (diagonal, below_block, upper_coupling_block, columns))
    elimination_ratios = stacked[:, :, :state_width]
    solved = stacked[:, :, state_width:]

    def backward(following, inputs):
        ratio_block, solved_block = inputs
        result = solved_block - product(ratio_block, following)
        return (result, result)
    _, answer = lax.scan(backward, jnp.zeros_like(columns[0]), (elimination_ratios, solved), reverse=True)
    return answer

def reference(dynamics, precision, right_side):
    state_width = dynamics.shape[1]
    identity = jnp.eye(state_width, dtype=dynamics.dtype)
    following = jnp.concatenate([dynamics[1:], jnp.zeros_like(dynamics[:1])], axis=0)
    diagonal = identity[None] + precision[:, :, None] * identity[None] + jnp.einsum('tki,tkj->tij', following, following, precision=lax.Precision.HIGHEST)
    below_block = (-dynamics).at[0].set(0.0)
    upper_coupling_block = -jnp.transpose(following, (0, 2, 1))
    columns = jnp.transpose(right_side, (0, 2, 1))
    states = block_thomas(diagonal, below_block, upper_coupling_block, columns)
    return jnp.transpose(states, (0, 2, 1))
```

```python
import jax
import jax.numpy as jnp
from jax import lax
from jax.experimental import pallas as pl
from jax.experimental.pallas import tpu as pltpu
from jax.sharding import PartitionSpec as P

F32 = jnp.float32
BF16 = jnp.bfloat16
STAGES = 3
ROBUST_STEPS = 48


def contract(left, right, nt, precision=None):
    return lax.dot_general(
        left,
        right,
        (((1,), (1 if nt else 0,)), ((), ())),
        precision=precision,
        preferred_element_type=F32,
    )


def by_rows(multiply, left):
    rows = left.shape[0]
    if rows < 32:
        return multiply(left)
    half = (rows // 2 + 7) // 8 * 8
    return jnp.concatenate([multiply(left[:half]), multiply(left[half:])], axis=0)


def exact(left, right, nt=False):
    return by_rows(lambda part: contract(part, right, nt, lax.Precision.HIGHEST), left)


def rough(left, right):
    return contract(left.astype(BF16), right.astype(BF16), False)


def high_and_rest(x):
    high = x.astype(BF16)
    return high, x - high.astype(F32)


def by_narrow(left, narrow):
    def multiply(part):
        high, rest = high_and_rest(part)
        middle, low = high_and_rest(rest)
        return contract(high, narrow, False) + (
            contract(middle, narrow, False) + contract(low.astype(BF16), narrow, False)
        )

    return by_rows(multiply, left)


def in_three(left, right):
    right_high, right_rest = high_and_rest(right)
    right_low = right_rest.astype(BF16)

    def multiply(part):
        high, rest = high_and_rest(part)
        return contract(high, right_high, False) + (
            contract(high, right_low, False) + contract(rest.astype(BF16), right_high, False)
        )

    return by_rows(multiply, left)


def stack(*parts):
    return jnp.concatenate(parts, axis=0)


def on_diagonal(width):
    return lax.broadcasted_iota(jnp.int32, (width, width), 0) == lax.broadcasted_iota(
        jnp.int32, (width, width), 1
    )


def quick_solve(pairs):
    width = pairs[0][0].shape[0]
    diagonal = on_diagonal(width)
    unit = jnp.where(diagonal, 1.0, 0.0).astype(F32)
    powers, sums, scales = [], [], []
    for matrix, _ in pairs:
        kept = jnp.where(diagonal, matrix, 0.0)
        error = unit - matrix * (1.0 / jnp.sum(kept, axis=0, keepdims=True))
        scales.append(1.0 / jnp.sum(kept, axis=1, keepdims=True))
        powers.append(error)
        sums.append(error)
    for stage in range(STAGES):
        squares = [rough(power, power) for power in powers] if stage + 1 < STAGES else None
        if stage > 0:
            sums = [
                total + power + rough(total, power) for total, power in zip(sums, powers)
            ]
        powers = squares
    narrow = [(scale * (unit + total)).astype(BF16) for scale, total in zip(scales, sums)]
    started = [by_narrow(stack(matrix, rows), near) for (matrix, rows), near in zip(pairs, narrow)]
    errors = [unit - both[:width] for both in started]
    squares = [rough(error, error) for error in errors]
    corrections = [
        error + square + rough(error, square) for error, square in zip(errors, squares)
    ]
    solved = [
        both[width:] + in_three(both[width:], correction)
        for both, correction in zip(started, corrections)
    ]
    left_over = sum(jnp.sum(square * square) for square in squares)
    return solved, left_over


def robust_solve(pairs, held):
    solved = []
    for matrix, rows in pairs:
        width = matrix.shape[0]
        diagonal = on_diagonal(width)
        unit = jnp.where(diagonal, 1.0, 0.0).astype(F32)
        kept = jnp.where(diagonal, matrix, 0.0)
        scaled = jnp.abs(matrix * (1.0 / jnp.sum(kept, axis=0, keepdims=True)))
        bound = jnp.max(jnp.sum(scaled, axis=0, keepdims=True))
        held[...] = unit * (1.0 / (bound * jnp.sum(kept, axis=1, keepdims=True)))

        def go_on(state):
            step, size = state
            return jnp.logical_and(step < ROBUST_STEPS, jnp.logical_not(size <= 1e-8))

        def improve(state):
            step, _ = state
            inverse = held[...]
            error = unit - exact(matrix, inverse)
            held[...] = inverse + exact(inverse, error)
            return step + 1, jnp.sum(error * error)

        lax.while_loop(go_on, improve, (jnp.int32(0), jnp.float32(1.0)))
        inverse = held[...]
        answer = exact(rows, inverse)
        solved.append(answer + exact(rows - exact(answer, matrix), inverse))
    return solved


def with_fallback(body, held):
    bounds = []

    def quick(pairs):
        solved, left_over = quick_solve(pairs)
        bounds.append(left_over)
        return solved

    body(quick)
    worst = sum(bounds)

    @pl.when(jnp.logical_not(worst <= 1e-6))
    def _():
        body(lambda pairs: robust_solve(pairs, held))


def choose(flag, when_true, when_false):
    return jnp.where(flag, when_true, when_false)


def leaf_parts(count, first, dynamics, precision, columns, has_before, has_after):
    left = dynamics[first]
    right = dynamics[first + 1]
    one = jnp.float32(1.0)
    if first == 0:
        left = left * has_before
    weight = jnp.ones_like(precision[first])
    source = columns[first]
    if first + 2 == count:
        after = precision[first + 1]
        shrunk = 1.0 / (one + after)
        weight = choose(has_after > 0, weight, after * shrunk)
        source = source + exact((1.0 - has_after) * columns[first + 1] * shrunk, right)
    left_t = left.T
    right_t = right.T
    eye = on_diagonal(left.shape[0])
    matrix = jnp.where(eye, one + precision[first], 0.0) + exact(right_t * weight, right)
    if first + 2 == count:
        right = right * has_after
    return left, left_t, right, matrix, source


def interior_kernel(dyn_ref, prec_ref, rhs_ref, flag_ref, near_ref, rest_ref, kept_ref, held):
    count, width = dyn_ref.shape[0], dyn_ref.shape[1]
    group = rhs_ref.shape[1]
    has_before = (flag_ref[0] > 0).astype(F32)
    has_after = (flag_ref[1] > 0).astype(F32)
    is_right = flag_ref[2] > 0
    eye = on_diagonal(width)

    def body(solve):
        dynamics = [dyn_ref[t] for t in range(count)]
        precision = [prec_ref[t : t + 1] for t in range(count)]
        columns = [rhs_ref[t] for t in range(count)]
        leaves = [
            leaf_parts(count, first, dynamics, precision, columns, has_before, has_after)
            for first in range(0, count, 2)
        ]
        pairs = [
            (matrix, stack(-left_t, -right, source)) for left, left_t, right, matrix, source in leaves
        ]
        solved = solve(pairs)
        elements = []
        for j, (leaf, answer) in enumerate(zip(leaves, solved)):
            left, left_t, right, _, _ = leaf
            first = 2 * j
            kept_ref[first] = answer
            to_left, to_right, own = answer[:width], answer[width : 2 * width], answer[2 * width :]
            edge = jnp.where(eye, 1.0 + precision[first + 1], 0.0)
            if j % 2 == 0:
                from_right = exact(answer, right, nt=True)
                from_left = exact(stack(left_t + to_left, own), left)
                coupling = from_right[:width]
                side = from_right[width:]
                low = from_left
            else:
                from_left = exact(stack(left_t + to_left, own, to_right), left)
                side = exact(stack(to_right, own), right, nt=True)
                low = from_left[: width + group]
                coupling = from_left[width + group :]
            left_part = (low[:width], low[width:])
            right_part = (edge + side[:width], columns[first + 1] + side[width:])
            far, near = (left_part, right_part) if j % 2 == 0 else (right_part, left_part)
            elements.append((near, coupling, far))
        first = 1
        while len(elements) > 1:
            pairs = []
            for j in range(0, len(elements), 2):
                one, other = elements[j], elements[j + 1]
                matrix = one[0][0] + other[0][0]
                pairs.append((matrix, stack(one[1], other[1], one[0][1] + other[0][1])))
            solved = solve(pairs)
            merged = []
            for j, answer in enumerate(solved):
                one, other = elements[2 * j], elements[2 * j + 1]
                kept_ref[first + 2 * (first + 1) * j] = answer
                last = len(solved) == 1
                turned = is_right if last else j % 2 == 1
                merged.append(join(answer, one, other, turned))
            elements = merged
            first = 2 * first + 1
        near, coupling, far = elements[0]
        near_ref[...] = stack(*near)
        rest_ref[...] = stack(coupling, *far)

    with_fallback(body, held)


def swapped(turned, first, second):
    if isinstance(turned, bool):
        return (second, first) if turned else (first, second)
    return choose(turned, second, first), choose(turned, first, second)


def join(answer, one, other, turned):
    width = answer.shape[1]
    one_rows, other_rows, own = answer[:width], answer[width : 2 * width], answer[2 * width :]
    one_change = exact(stack(one_rows, own), one[1], nt=True)
    other_change = exact(stack(other_rows, own), other[1], nt=True)
    far_rows, _ = swapped(turned, one_rows, other_rows)
    _, near_coupling = swapped(turned, one[1], other[1])
    coupling = -exact(far_rows, near_coupling, nt=True)
    one_end = (one[2][0] - one_change[:width], one[2][1] - one_change[width:])
    other_end = (other[2][0] - other_change[:width], other[2][1] - other_change[width:])
    far_matrix, near_matrix = swapped(turned, one_end[0], other_end[0])
    far_source, near_source = swapped(turned, one_end[1], other_end[1])
    return (near_matrix, near_source), coupling, (far_matrix, far_source)


def unpack(near_ref, rest_ref):
    width = near_ref.shape[1]
    near = (near_ref[:width], near_ref[width:])
    far = (rest_ref[width : 2 * width], rest_ref[2 * width :])
    return near, rest_ref[:width], far


def merge_kernel(
    own_near_ref, own_rest_ref, got_near_ref, got_rest_ref, flag_ref,
    near_ref, rest_ref, kept_ref, held,
):
    keeps = flag_ref[0] > 0

    def body(solve):
        own = unpack(own_near_ref, own_rest_ref)
        got = unpack(got_near_ref, got_rest_ref)
        matrix = own[0][0] + got[0][0]
        source = own[0][1] + got[0][1]
        (answer,) = solve([(matrix, stack(own[1], got[1], source))])
        near, coupling, far = join(answer, own, got, jnp.logical_not(keeps))
        kept_ref[...] = answer
        near_ref[...] = stack(*near)
        rest_ref[...] = stack(coupling, *far)

    with_fallback(body, held)


def outer_merge_kernel(
    own_near_ref, own_rest_ref, got_near_ref, got_rest_ref, flag_ref, near_ref, kept_ref, held
):
    keeps = flag_ref[0] > 0
    width = own_near_ref.shape[1]

    def body(solve):
        own = unpack(own_near_ref, own_rest_ref)
        got = unpack(got_near_ref, got_rest_ref)
        matrix = own[0][0] + got[0][0]
        source = own[0][1] + got[0][1]
        coupling = choose(keeps, got[1], own[1])
        far_matrix = choose(keeps, got[2][0], own[2][0])
        far_source = choose(keeps, got[2][1], own[2][1])
        (answer,) = solve([(matrix, stack(coupling, source))])
        change = exact(answer, coupling, nt=True)
        kept_ref[...] = answer
        near_ref[...] = stack(far_matrix - change[:width], far_source - change[width:])

    with_fallback(body, held)


def finish_kernel(levels, *refs):
    own_ref, got_ref, dyn_ref, prec_ref, rhs_ref, flag_ref, inner_ref = refs[:7]
    kept_refs = refs[7 : 7 + levels]
    out_ref, held = refs[7 + levels :]
    count = inner_ref.shape[0] + 1
    width = own_ref.shape[1]
    has_after = flag_ref[0] > 0

    def body(solve):
        matrix = own_ref[:width] + got_ref[:width]
        source = own_ref[width:] + got_ref[width:]
        (top,) = solve([(matrix, source)])
        near, far = top, jnp.zeros_like(top)
        for level in reversed(range(levels)):
            kept = kept_refs[level]
            if kept.shape[0] < 2 * width:
                state = kept[width:] - exact(near, kept[:width])
            else:
                keeps = flag_ref[1 + level] > 0
                own_end, got_end = choose(keeps, far, near), choose(keeps, near, far)
                ends = jnp.concatenate([own_end, got_end], axis=1)
                state = kept[2 * width :] - exact(ends, kept[: 2 * width])
            keeps = flag_ref[1 + level] > 0
            far = choose(keeps, far, near)
            near = state
        is_right = flag_ref[1 + levels] > 0
        states = {-1: choose(is_right, near, far), count - 1: choose(is_right, far, near)}
        step = count // 2
        while step >= 1:
            for middle in range(step - 1, count - 1, 2 * step):
                ends = jnp.concatenate([states[middle - step], states[middle + step]], axis=1)
                kept = inner_ref[middle]
                states[middle] = kept[2 * width :] - exact(ends, kept[: 2 * width])
            step //= 2
        last = (
            rhs_ref[count - 1] + exact(states[count - 2], dyn_ref[...], nt=True)
        ) * (1.0 / (1.0 + prec_ref[count - 1 : count]))
        states[count - 1] = choose(has_after, states[count - 1], last)
        for t in range(count):
            out_ref[t] = states[t]

    with_fallback(body, held)


def smem():
    return pl.BlockSpec(memory_space=pltpu.SMEM)


def vmem():
    return pl.BlockSpec(memory_space=pltpu.VMEM)


def exchanged(x, axis, distance):
    pairs = [(i, i ^ distance) for i in range(lax.axis_size(axis))]
    return lax.ppermute(x, axis, pairs)


def local(dynamics, precision, right_side):
    count, width = dynamics.shape[0], dynamics.shape[1]
    group = right_side.shape[1]
    size = lax.axis_size("tm")
    levels = size.bit_length() - 1
    assert size == 1 << levels and levels >= 2 and count & (count - 1) == 0 and count >= 4
    index = lax.axis_index("tm")
    bits = [(index >> level) & 1 for level in range(levels)]
    keeps = [(bits[level] == bits[level + 1]).astype(jnp.int32) for level in range(levels - 1)]
    has_before = (index > 0).astype(jnp.int32)
    has_after = (index < size - 1).astype(jnp.int32)
    held = [pltpu.VMEM((width, width), F32)]
    near_shape = jax.ShapeDtypeStruct((width + group, width), F32)
    rest_shape = jax.ShapeDtypeStruct((2 * width + group, width), F32)
    near, rest, inner = pl.pallas_call(
        interior_kernel,
        out_shape=(
            near_shape,
            rest_shape,
            jax.ShapeDtypeStruct((count - 1, 2 * width + group, width), F32),
        ),
        in_specs=[vmem(), vmem(), vmem(), smem()],
        out_specs=(vmem(), vmem(), vmem()),
        scratch_shapes=held,
        name="interior",
    )(dynamics, precision, right_side, jnp.stack([has_before, has_after, bits[0]]))
    kept = []
    for level in range(levels - 1):
        got_near = exchanged(near, "tm", 1 << level)
        got_rest = exchanged(rest, "tm", 1 << level)
        last = level == levels - 2
        flags = keeps[level][None]
        if last:
            near, answer = pl.pallas_call(
                outer_merge_kernel,
                out_shape=(near_shape, near_shape),
                in_specs=[vmem()] * 4 + [smem()],
                out_specs=(vmem(), vmem()),
                scratch_shapes=held,
                name="outer",
            )(near, rest, got_near, got_rest, flags)
        else:
            near, rest, answer = pl.pallas_call(
                merge_kernel,
                out_shape=(near_shape, rest_shape, rest_shape),
                in_specs=[vmem()] * 4 + [smem()],
                out_specs=(vmem(), vmem(), vmem()),
                scratch_shapes=held,
                name="merge",
            )(near, rest, got_near, got_rest, flags)
        kept.append(answer)
    got = exchanged(near, "tm", 1 << (levels - 1))
    flags = jnp.stack([has_after, *keeps, bits[0]])
    return pl.pallas_call(
        lambda *refs: finish_kernel(levels - 1, *refs),
        out_shape=jax.ShapeDtypeStruct(right_side.shape, F32),
        in_specs=[vmem()] * 5 + [smem()] + [vmem()] * (len(kept) + 1),
        out_specs=vmem(),
        scratch_shapes=held,
        name="finish",
    )(near, got, dynamics[count - 1], precision, right_side, flags, inner, *kept)


def solution(mesh):
    return jax.shard_map(
        local,
        mesh=mesh,
        in_specs=(P("tm", None, None), P("tm", None), P("tm", "ens", None)),
        out_specs=P("tm", "ens", None),
        check_vma=False,
    )
```
